128 devices in a mesh: row: 8 (over z_hi, x), col: 16 (over y, z_lo, core).
Axes of the slice: x: 4, y: 4, z: 4 (z_hi: 2, z_lo: 2; z = z_hi * 2 + z_lo), core: 2. Of those that a mesh axis runs over, the one named last changes fastest.
Arguments:
- kernel_blocks: bfloat16 [64, 8, 256, 256], P('col', 'row'), may hold values from -6 to 6
- row_intersection: bfloat16 [512, 256, 256], P('col'), may hold values from -0.375 to 0.375
- col_intersection: bfloat16 [32, 256, 256], P('row'), may hold values from -0.375 to 0.375
- trial: bfloat16 [32, 64, 256], P('row', 'col'), may hold values from -0.0625 to 0.0625
- coarse_of_row: int32 [512], replicated, may hold values from 0 to 63, as said below
Outputs:
- fine_kernel: bfloat16 [512, 32, 256, 256], P('col', 'row')
- applied: bfloat16 [512, 64, 256], P(('col', 'row'))
The draws below stay inside these ranges and needn't reach their ends.
Inputs may be any that keep to these rules, and one draw needn't show every extreme that they name: coarse_of_row never falls from one fine point to the next; coarse point 0 starts at fine point 0, and coarse point j >= 1 starts at fine point j * 8 - 512 // 128 + e_j with e_j between -3 and 3; every coarse point takes 1 to 15 consecutive fine points, and the last takes exactly 15.
All inputs are finite; a program needn't handle non-finite values.
Results may differ from the reference program's by a relative error of at most 0.0057.
Values may be sent and summed in bfloat16 or wider, within the bound.
A program may use at most 128 MiB of HBM per device.

```python
import jax
import jax.numpy as jnp
from jax import lax

NK = 512
P_SIZE = 256
NV = 64
NC = 64
COLS_DEV = 4
CW = 8
COLS = 32


def draw_coarse_of_row(key, part):
    spacing = NK // NC
    jitter = jax.random.randint(jax.random.fold_in(key, 7), (NC,), -3, 4).astype(jnp.int32)
    jitter = jitter.at[NC - 1].set(-3)
    points = jnp.arange(NC, dtype=jnp.int32)
    starts = points * spacing - spacing // 2 + jitter
    starts = starts[1:]
    fine = jnp.arange(NK, dtype=jnp.int32)
    return jnp.sum((fine[:, None] >= starts[None, :]).astype(jnp.int32), axis=1).astype(jnp.int32)


def level_of(rng, extent, shards, smallest, high):
    gain, own = 1.0, jax.random.fold_in(rng, 6)
    for position, shards_of in shards:
        steps = jnp.exp(jax.random.uniform(jax.random.fold_in(own, position), (shards_of,), jnp.float32, smallest / len(shards), high / len(shards)))
        gain = gain * jnp.repeat(steps, extent[position] // shards_of).reshape([-1 if axis == position else 1 for axis in range(len(extent))])
    return gain


def bell_draw(key, extent, deviation, reach, cuts=(), held_as=jnp.bfloat16):
    values = deviation * jax.random.normal(key, extent, jnp.float32)
    if cuts:
        values = values * level_of(key, extent, cuts, -0.22, 0.18)
    return jnp.clip(values, -reach, reach).astype(held_as)


def setup_inputs(seed: int = 0) -> dict:
    splits = jax.random.split(jax.random.key(seed), 6)
    return {
        "kernel_blocks": bell_draw(splits[0], (NC, CW, P_SIZE, P_SIZE), 1.0, 6.0, ((0, 16), (1, 8))),
        "row_intersection": bell_draw(splits[1], (NK, P_SIZE, P_SIZE), P_SIZE ** -0.5, 0.375, ((0, 16),)),
        "col_intersection": bell_draw(splits[2], (COLS, P_SIZE, P_SIZE), P_SIZE ** -0.5, 0.375, ((0, 8),)),
        "trial": bell_draw(splits[3], (COLS, NV, P_SIZE), (COLS * P_SIZE) ** -0.5, 0.0625, ((0, 8), (1, 16))),
        "coarse_of_row": draw_coarse_of_row(jax.random.fold_in(splits[5], 71), 0),
    }


def reference(kernel_blocks, row_intersection, col_intersection, trial, coarse_of_row):
    intersection_wide = col_intersection.astype(jnp.float32)
    trial_wide = trial.astype(jnp.float32)

    def right_of(block_row):
        spread = jnp.repeat(block_row, COLS_DEV, axis=0).astype(jnp.float32)
        return jnp.einsum("jab,jbc->jac", spread, intersection_wide).astype(jnp.bfloat16)

    right_all = lax.map(right_of, kernel_blocks)

    def one_row(items):
        index, urow = items
        picked = lax.dynamic_index_in_dim(right_all, index.astype(jnp.int32), 0, keepdims=False).astype(jnp.float32)
        fine = jnp.einsum("ba,jbc->jac", urow.astype(jnp.float32), picked).astype(jnp.bfloat16)
        part = jnp.einsum("jab,jvb->va", fine.astype(jnp.float32), trial_wide).astype(jnp.bfloat16)
        return fine, part

    fine_kernel, applied = lax.map(one_row, (coarse_of_row, row_intersection))
    return fine_kernel, applied
```

```python
import jax
import jax.numpy as jnp
from jax import lax
from jax.experimental import pallas as pl
from jax.experimental.pallas import tpu as pltpu
from jax.sharding import PartitionSpec as P

MESH = pl.DeviceIdType.MESH
BF = jnp.bfloat16
F32 = jnp.float32
NROW, NCOL = 8, 16
S = 256
NV = 64
KD = 32
MD = 4
NB = 5


def split_halves(x):
    high = x.astype(BF)
    return high, (x - high.astype(F32)).astype(BF)


def dot_t(x, y):
    return lax.dot_general(x, y, (((1,), (1,)), ((), ())), preferred_element_type=F32)


def exchange(
    kb_ref, ci_ref, tr_ref, right_ref, w_ref,
    kbuf, cbuf, tbuf, ypart, ybuf, pbuf, wbuf,
    lsem, ksend, krecv, ysend, yrecv, wsend, wrecv,
):
    r = lax.axis_index("row")
    c = lax.axis_index("col")

    load_t = pltpu.make_async_copy(tr_ref, tbuf, lsem.at[0])
    load_c = pltpu.make_async_copy(ci_ref, cbuf, lsem.at[1])
    load_k = pltpu.make_async_copy(kb_ref.at[:, 0], kbuf.at[pl.ds(0, 4)], lsem.at[2])
    load_t.start()
    load_c.start()
    load_k.start()

    barrier = pltpu.get_barrier_semaphore()

    @pl.loop(1, NCOL)
    def _(off):
        pl.semaphore_signal(barrier, inc=1, device_id={"col": lax.rem(c + off, NCOL)}, device_id_type=MESH)

    @pl.loop(1, NROW)
    def _(off):
        pl.semaphore_signal(barrier, inc=1, device_id={"row": lax.rem(r + off, NROW)}, device_id_type=MESH)

    load_t.wait()
    load_c.wait()
    y = dot_t(tbuf[0], cbuf[0])
    for m in range(1, MD):
        y += dot_t(tbuf[m], cbuf[m])
    high, low = split_halves(y)
    both = jnp.concatenate([high.astype(F32), low.astype(F32)], axis=0).astype(BF)
    ypart[...] = both
    ybuf[c] = both
    load_k.wait()

    pl.semaphore_wait(barrier, NCOL + NROW - 2)

    def k_copy():
        return pltpu.make_async_remote_copy(
            src_ref=kbuf.at[0], dst_ref=kbuf.at[4], send_sem=ksend, recv_sem=krecv,
            device_id={"col": lax.rem(c + NCOL - 1, NCOL)}, device_id_type=MESH,
        )

    def y_copy(off):
        return pltpu.make_async_remote_copy(
            src_ref=ypart, dst_ref=ybuf.at[c], send_sem=ysend.at[off], recv_sem=yrecv.at[c],
            device_id={"col": lax.rem(c + off, NCOL)}, device_id_type=MESH,
        )

    def y_arrival(off):
        return pltpu.make_async_remote_copy(
            src_ref=ypart, dst_ref=ybuf.at[lax.rem(c + off, NCOL)], send_sem=ysend.at[off],
            recv_sem=yrecv.at[lax.rem(c + off, NCOL)],
            device_id={"col": lax.rem(c + off, NCOL)}, device_id_type=MESH,
        )

    @pl.loop(1, NCOL)
    def _(off):
        y_copy(off).start()

    k_copy().start()

    @pl.loop(0, 4)
    def _(p):
        for m in range(MD):
            right_ref[p, :, m * S:(m + 1) * S] = jnp.dot(
                kbuf[p], cbuf[m], preferred_element_type=F32
            ).astype(BF)

    @pl.loop(1, NCOL)
    def _(off):
        y_arrival(off).wait_recv()

    yall = ybuf[...].astype(F32).reshape(NCOL * 8, S).astype(BF)

    def partial(p):
        x = dot_t(yall, kbuf[p]).reshape(NCOL // 2, 2, 8, S)
        x = x + jnp.concatenate([x[:, :, 4:], x[:, :, :4]], axis=2)
        first = lax.broadcasted_iota(jnp.int32, (NCOL // 2, 8, S), 1) < 4
        return jnp.where(first, x[:, 0], x[:, 1]).reshape(NV, S)

    k_copy().wait_recv()

    @pl.loop(0, NB)
    def _(p):
        pbuf[p] = partial(p).astype(BF)

    def w_copy(off):
        d = lax.rem(r + off, NROW)
        return pltpu.make_async_remote_copy(
            src_ref=pbuf.at[pl.ds(d // 2, 2)], dst_ref=wbuf.at[r], send_sem=wsend.at[off], recv_sem=wrecv.at[r],
            device_id={"row": d}, device_id_type=MESH,
        )

    def w_arrival(off):
        d = lax.rem(r + off, NROW)
        return pltpu.make_async_remote_copy(
            src_ref=pbuf.at[pl.ds(d // 2, 2)], dst_ref=wbuf.at[d], send_sem=wsend.at[off], recv_sem=wrecv.at[d],
            device_id={"row": d}, device_id_type=MESH,
        )

    @pl.loop(1, NROW)
    def _(off):
        w_copy(off).start()

    for m in range(MD):
        right_ref[4, :, m * S:(m + 1) * S] = jnp.dot(kbuf[4], cbuf[m], preferred_element_type=F32).astype(BF)
    wbuf[r] = pbuf[pl.ds(r // 2, 2)]

    k_copy().wait_send()

    @pl.loop(1, NCOL)
    def _(off):
        y_copy(off).wait_send()

    @pl.loop(1, NROW)
    def _(off):
        w_arrival(off).wait_recv()

    total = wbuf[0].astype(F32)
    for i in range(1, NROW):
        total += wbuf[i].astype(F32)
    w_ref[...] = total

    @pl.loop(1, NROW)
    def _(off):
        w_copy(off).wait_send()


def expand(cor_ref, row_ref, right_ref, w_ref, fine_ref, app_ref, wsplit):
    step = pl.program_id(0)
    r = lax.axis_index("row")
    c = lax.axis_index("col")
    position = jnp.clip(cor_ref[c * KD + step] - c * 4, 0, NB - 1)
    rows = row_ref[0]
    out = lax.dot_general(
        rows, right_ref[position], (((0,), (0,)), ((), ())), preferred_element_type=F32
    ).astype(BF)
    for m in range(MD):
        fine_ref[0, m] = out[:, m * S:(m + 1) * S]

    @pl.when(step == 0)
    def _():
        for i in range(2):
            high, low = split_halves(w_ref[i])
            wsplit[i, :NV] = high
            wsplit[i, NV:] = low

    @pl.when(step // 4 == r)
    def _():
        which = jnp.clip(position - r // 2, 0, 1)
        x = jnp.dot(wsplit[which], rows, preferred_element_type=F32)
        app_ref[step % 4] = (x[:NV] + x[NV:]).astype(BF)


def per_device(kernel_blocks, row_intersection, col_intersection, trial, coarse_of_row):
    hbm_spec = pl.BlockSpec(memory_space=pltpu.HBM)
    vmem_spec = pl.BlockSpec(memory_space=pltpu.VMEM)
    right, w = pl.pallas_call(
        exchange,
        out_shape=(jax.ShapeDtypeStruct((NB, S, MD * S), BF), jax.ShapeDtypeStruct((2, NV, S), F32)),
        in_specs=[hbm_spec, hbm_spec, hbm_spec],
        out_specs=(vmem_spec, vmem_spec),
        scratch_shapes=[
            pltpu.VMEM((NB, S, S), BF),
            pltpu.VMEM((MD, S, S), BF),
            pltpu.VMEM((MD, 4, S), BF),
            pltpu.VMEM((8, S), BF),
            pltpu.VMEM((NCOL, 8, S), BF),
            pltpu.VMEM((NB, NV, S), BF),
            pltpu.VMEM((NROW, 2, NV, S), BF),
            pltpu.SemaphoreType.DMA((3,)),
            pltpu.SemaphoreType.DMA,
            pltpu.SemaphoreType.DMA,
            pltpu.SemaphoreType.DMA((NCOL,)),
            pltpu.SemaphoreType.DMA((NCOL,)),
            pltpu.SemaphoreType.DMA((NROW,)),
            pltpu.SemaphoreType.DMA((NROW,)),
        ],
        compiler_params=pltpu.CompilerParams(
            collective_id=0, has_side_effects=True, vmem_limit_bytes=16 << 20
        ),
        name="exchange",
    )(kernel_blocks, col_intersection, trial)

    return pl.pallas_call(
        expand,
        out_shape=(jax.ShapeDtypeStruct((KD, MD, S, S), BF), jax.ShapeDtypeStruct((4, NV, S), BF)),
        grid_spec=pltpu.PrefetchScalarGridSpec(
            num_scalar_prefetch=1,
            grid=(KD,),
            in_specs=[
                pl.BlockSpec((1, S, S), lambda k, cor: (k, 0, 0)),
                pl.BlockSpec((NB, S, MD * S), lambda k, cor: (0, 0, 0), pipeline_mode=pl.Buffered(1)),
                pl.BlockSpec((2, NV, S), lambda k, cor: (0, 0, 0), pipeline_mode=pl.Buffered(1)),
            ],
            out_specs=(
                pl.BlockSpec((1, MD, S, S), lambda k, cor: (k, 0, 0, 0)),
                pl.BlockSpec((4, NV, S), lambda k, cor: (0, 0, 0)),
            ),
            scratch_shapes=[pltpu.VMEM((2, 2 * NV, S), BF)],
        ),
        compiler_params=pltpu.CompilerParams(
            dimension_semantics=("arbitrary",), vmem_limit_bytes=16 << 20
        ),
        name="expand",
    )(coarse_of_row, row_intersection, right, w)


def solution(mesh):
    in_specs = (
        P("col", "row", None, None),
        P("col", None, None),
        P("row", None, None),
        P("row", "col", None),
        P(),
    )
    out_specs = (P("col", "row", None, None), P(("col", "row"), None, None))
    return jax.shard_map(
        per_device, mesh=mesh, in_specs=in_specs, out_specs=out_specs, check_vma=False
    )
```

```python
import jax
import jax.numpy as jnp
from jax import lax
from jax.experimental import pallas as pl
from jax.experimental.pallas import tpu as pltpu
from jax.sharding import PartitionSpec as P

MESH = pl.DeviceIdType.MESH
BF = jnp.bfloat16
F32 = jnp.float32
NROW, NCOL = 8, 16
S = 256
NV = 64
KD = 32
MD = 4
NB = 5
CUTS = (0, 8, 10, 20)
EARLY = CUTS[-1]
NEAR = 48
COL_ORDER = [(dy, dj) for dy in (2, 1, 3, 0) for dj in range(4) if dy or dj]
ROW_ORDER = [(1, 2), (1, 1), (1, 3), (1, 0), (0, 2), (0, 1), (0, 3)]


def split_halves(x):
    high = x.astype(BF)
    return high, (x - high.astype(F32)).astype(BF)


def fine_block(rows, right):
    return lax.dot_general(rows, right, (((0,), (0,)), ((), ())), preferred_element_type=F32).astype(BF)


def remote(src, dst, send_sem, recv_sem, **device):
    return pltpu.make_async_remote_copy(
        src_ref=src, dst_ref=dst, send_sem=send_sem, recv_sem=recv_sem, device_id=device, device_id_type=MESH
    )


def exchange(
    cor_ref, kb_ref, ci_ref, tr_ref, row_ref, fine_ref, right_ref, rows_ref, w_ref,
    cor, kbuf, kt, cbuf, tbuf, ypart, ybuf, pbuf, wbuf,
    lsem, ksend, krecv, ysend, yrecv, wsend, wrecv,
):
    r = lax.axis_index("row")
    c = lax.axis_index("col")
    y, j = c // 4, lax.rem(c, 4)

    load_t = pltpu.make_async_copy(tr_ref, tbuf, lsem.at[0])
    load_c = pltpu.make_async_copy(ci_ref, cbuf, lsem.at[1])
    load_k = pltpu.make_async_copy(kb_ref.at[:, 0], kbuf.at[pl.ds(0, 4)], lsem.at[2])
    load_p = pltpu.make_async_copy(cor_ref, cor, lsem.at[3])
    load_r = pltpu.make_async_copy(row_ref, rows_ref, lsem.at[4])
    load_t.start()
    load_c.start()
    load_k.start()

    col_peers = [lax.rem(y + dy, 4) * 4 + lax.rem(j + dj, 4) for dy, dj in COL_ORDER]
    row_peers = [lax.rem(r // 4 + dz, 2) * 4 + lax.rem(lax.rem(r, 4) + dx, 4) for dz, dx in ROW_ORDER]
    barrier = pltpu.get_barrier_semaphore()
    for peer in row_peers:
        pl.semaphore_signal(barrier, inc=1, device_id={"row": peer}, device_id_type=MESH)
    for peer in col_peers:
        pl.semaphore_signal(barrier, inc=1, device_id={"col": peer}, device_id_type=MESH)
    load_p.start()
    load_r.start()

    load_t.wait()
    load_c.wait()
    part = None
    for m in range(MD):
        x = lax.dot_general(tbuf[m], cbuf[m], (((1,), (1,)), ((), ())), preferred_element_type=F32)
        part = x if part is None else part + x
    high, low = split_halves(part)
    both = jnp.concatenate([high.astype(F32), low.astype(F32)], axis=0).astype(BF)
    ypart[...] = both
    ybuf[1, j] = both
    load_k.wait()

    def right_block(p):
        for m in range(MD):
            right_ref[p, :, m * S:(m + 1) * S] = jnp.dot(kbuf[p], cbuf[m], preferred_element_type=F32).astype(BF)

    @pl.loop(0, 4)
    def _(p):
        kt[p] = kbuf[p].T
        right_block(p)

    pl.semaphore_wait(barrier, NCOL + NROW - 2)

    k_copy = remote(kbuf.at[0], kbuf.at[4], ksend, krecv, col=lax.rem(c + NCOL - 1, NCOL))
    y_copies = []
    for i, ((dy, dj), peer) in enumerate(zip(COL_ORDER, col_peers)):
        slot = (1 - dy) % 4
        y_copies.append(remote(ypart, ybuf.at[slot, j], ysend.at[i], yrecv.at[slot, j], col=peer))
    for copy in y_copies:
        copy.start()
    k_copy.start()

    def wait_y(slots):
        for slot in slots:
            for dj in range(4):
                if slot != 1 or dj:
                    other = lax.rem(j + dj, 4)
                    remote(ypart, ybuf.at[slot, other], ysend.at[0], yrecv.at[slot, other], col=c).wait_recv()

    def fine_range(start, stop):
        @pl.loop(start, stop, step=2)
        def _(k):
            for i in range(2):
                position = jnp.clip(cor[c * KD + k + i] - c * 4, 0, NB - 1)
                out = fine_block(rows_ref[k + i], right_ref[position])
                for m in range(MD):
                    fine_ref[k + i, m] = out[:, m * S:(m + 1) * S]

    def partial(left, p):
        n = left.shape[0] // 16
        x = jnp.dot(left, kt[p], preferred_element_type=F32).reshape(n, 2, 8, S)
        x = x + jnp.concatenate([x[:, :, 4:], x[:, :, :4]], axis=2)
        first = lax.broadcasted_iota(jnp.int32, (n, 8, S), 1) < 4
        return jnp.where(first, x[:, 0], x[:, 1]).reshape(n * 8, S).astype(BF)

    load_p.wait()
    load_r.wait()
    fine_range(CUTS[0], CUTS[1])

    wait_y((1, 0, 2))
    left_near = ybuf[0:3].astype(F32).reshape(96, S).astype(BF)
    for p in range(4):
        pbuf[p, 0:NEAR] = partial(left_near, p)

    for i, d in enumerate(row_peers):
        q = d // 2

        @pl.when(q < 3)
        def _():
            remote(
                pbuf.at[pl.ds(q, 2), pl.ds(0, NEAR)], wbuf.at[r, :, pl.ds(0, NEAR)], wsend.at[i], wrecv.at[r], row=d
            ).start()

        @pl.when(q == 3)
        def _():
            remote(
                pbuf.at[3, pl.ds(0, NEAR)], wbuf.at[r, 0, pl.ds(0, NEAR)], wsend.at[i], wrecv.at[r], row=d
            ).start()

    fine_range(CUTS[1], CUTS[2])
    k_copy.wait_recv()
    kt[4] = kbuf[4].T
    pbuf[4, 0:NEAR] = partial(left_near, 4)

    wait_y((3,))
    left_far = ybuf[3].astype(F32).reshape(32, S).astype(BF)
    for p in range(NB):
        pbuf[p, NEAR:] = partial(left_far, p)

    for i, d in enumerate(row_peers):
        q = d // 2

        @pl.when(q < 3)
        def _():
            remote(
                pbuf.at[pl.ds(q, 2), pl.ds(NEAR, NV - NEAR)], wbuf.at[r, :, pl.ds(NEAR, NV - NEAR)],
                wsend.at[i], wrecv.at[r], row=d,
            ).start()

        @pl.when(q == 3)
        def _():
            remote(pbuf.at[4], wbuf.at[r, 1], wsend.at[i], wrecv.at[r], row=d).start()
            remote(
                pbuf.at[3, pl.ds(NEAR, NV - NEAR)], wbuf.at[r, 0, pl.ds(NEAR, NV - NEAR)],
                wsend.at[i], wrecv.at[r], row=d,
            ).start()

    right_block(4)
    fine_range(CUTS[2], CUTS[3])

    k_copy.wait_send()
    for copy in y_copies:
        copy.wait_send()
    total = pbuf[pl.ds(r // 2, 2)].astype(F32)
    for d in reversed(row_peers):
        remote(wbuf.at[d], wbuf.at[d], wsend.at[0], wrecv.at[d], row=d).wait_recv()
        total += wbuf[d].astype(F32)
    for slot in range(4):
        w_ref[:, lax.rem(y + 3 + slot, 4)] = total[:, slot * 16:(slot + 1) * 16]
    for i, d in enumerate(row_peers):
        remote(pbuf.at[pl.ds(d // 2, 2)], wbuf.at[d], wsend.at[i], wrecv.at[d], row=d).wait_send()


def finish(
    cor_ref, early_ref, right_ref, rows_ref, w_ref, fine_ref, app_ref, cor, late, app, wsplit, sem, esem, lsem, asem
):
    r = lax.axis_index("row")
    c = lax.axis_index("col")
    load_p = pltpu.make_async_copy(cor_ref, cor, sem)
    load_p.start()
    early = [
        pltpu.make_async_copy(early_ref.at[pl.ds(i * 4, 4)], fine_ref.at[pl.ds(i * 4, 4)], esem.at[i])
        for i in range(EARLY // 4)
    ]
    for copy in early:
        copy.start()
    for i in range(2):
        high, low = split_halves(w_ref[i].reshape(NV, S))
        wsplit[i, :NV] = high
        wsplit[i, NV:] = low
    load_p.wait()

    def position_of(k):
        return jnp.clip(cor[c * KD + k] - c * 4, 0, NB - 1)

    def late_copy(k):
        return pltpu.make_async_copy(late.at[pl.ds(k, 2)], fine_ref.at[pl.ds(EARLY + k, 2)], lsem.at[k // 2])

    @pl.loop(0, KD - EARLY, step=2)
    def _(k):
        for i in range(2):
            out = fine_block(rows_ref[EARLY + k + i], right_ref[position_of(EARLY + k + i)])
            for m in range(MD):
                late[k + i, m] = out[:, m * S:(m + 1) * S]
        late_copy(k).start()

    for i in range(4):
        k = r * 4 + i
        which = jnp.clip(position_of(k) - r // 2, 0, 1)
        x = jnp.dot(wsplit[which], rows_ref[k], preferred_element_type=F32)
        app[i] = (x[:NV] + x[NV:]).astype(BF)
    app_copy = pltpu.make_async_copy(app, app_ref, asem)
    app_copy.start()

    for copy in early:
        copy.wait()

    @pl.loop(0, KD - EARLY, step=2)
    def _(k):
        late_copy(k).wait()

    app_copy.wait()


def per_device(kernel_blocks, row_intersection, col_intersection, trial, coarse_of_row):
    hbm_spec = pl.BlockSpec(memory_space=pltpu.HBM)
    vmem_spec = pl.BlockSpec(memory_space=pltpu.VMEM)
    arrays = (coarse_of_row, kernel_blocks, col_intersection, trial, row_intersection)
    arrays = [pltpu.with_memory_space_constraint(x, pltpu.HBM) for x in arrays]
    early, right, rows, w = pl.pallas_call(
        exchange,
        out_shape=(
            jax.ShapeDtypeStruct((EARLY, MD, S, S), BF),
            jax.ShapeDtypeStruct((NB, S, MD * S), BF),
            jax.ShapeDtypeStruct((KD, S, S), BF),
            jax.ShapeDtypeStruct((2, 4, 16, S), F32),
        ),
        in_specs=[hbm_spec] * 5,
        out_specs=(vmem_spec,) * 4,
        scratch_shapes=[
            pltpu.SMEM((NCOL * KD,), jnp.int32),
            pltpu.VMEM((NB, S, S), BF),
            pltpu.VMEM((NB, S, S), BF),
            pltpu.VMEM((MD, S, S), BF),
            pltpu.VMEM((MD, 4, S), BF),
            pltpu.VMEM((8, S), BF),
            pltpu.VMEM((4, 4, 8, S), BF),
            pltpu.VMEM((NB, NV, S), BF),
            pltpu.VMEM((NROW, 2, NV, S), BF),
            pltpu.SemaphoreType.DMA((5,)),
            pltpu.SemaphoreType.DMA,
            pltpu.SemaphoreType.DMA,
            pltpu.SemaphoreType.DMA((NCOL,)),
            pltpu.SemaphoreType.DMA((4, 4)),
            pltpu.SemaphoreType.DMA((NROW,)),
            pltpu.SemaphoreType.DMA((NROW,)),
        ],
        compiler_params=pltpu.CompilerParams(
            collective_id=0, has_side_effects=True, vmem_limit_bytes=28 << 20
        ),
        name="exchange",
    )(*arrays)

    return pl.pallas_call(
        finish,
        out_shape=(jax.ShapeDtypeStruct((KD, MD, S, S), BF), jax.ShapeDtypeStruct((4, NV, S), BF)),
        in_specs=[hbm_spec] + [vmem_spec] * 4,
        out_specs=(hbm_spec, hbm_spec),
        scratch_shapes=[
            pltpu.SMEM((NCOL * KD,), jnp.int32),
            pltpu.VMEM((KD - EARLY, MD, S, S), BF),
            pltpu.VMEM((4, NV, S), BF),
            pltpu.VMEM((2, 2 * NV, S), BF),
            pltpu.SemaphoreType.DMA,
            pltpu.SemaphoreType.DMA((EARLY // 4,)),
            pltpu.SemaphoreType.DMA(((KD - EARLY) // 2,)),
            pltpu.SemaphoreType.DMA,
        ],
        compiler_params=pltpu.CompilerParams(vmem_limit_bytes=28 << 20),
        name="finish",
    )(arrays[0], early, right, rows, w)


def solution(mesh):
    in_specs = (
        P("col", "row", None, None),
        P("col", None, None),
        P("row", None, None),
        P("row", "col", None),
        P(),
    )
    out_specs = (P("col", "row", None, None), P(("col", "row"), None, None))
    return jax.shard_map(
        per_device, mesh=mesh, in_specs=in_specs, out_specs=out_specs, check_vma=False
    )
```

```python
import jax
import jax.numpy as jnp
from jax import lax
from jax.experimental import pallas as pl
from jax.experimental.pallas import tpu as pltpu
from jax.sharding import PartitionSpec as P

MESH = pl.DeviceIdType.MESH
BF = jnp.bfloat16
F32 = jnp.float32
NROW, NCOL = 8, 16
S = 256
NV = 64
KD = 32
MD = 4
NB = 5
CUTS = (0, 4, 8, 16)
EARLY = CUTS[-1]
NEAR = 56
UNITS = ((0, 0), (3, 0), (1, 0), (0, 1), (2, 0), (3, 1), (1, 1), (2, 1))
COL_ORDER = [
    (dy, flip, dc)
    for dy, flip in ((2, 1), (1, 1), (3, 1), (2, 0), (0, 1), (1, 0), (3, 0), (0, 0))
    for dc in range(2)
    if dy or flip or dc
]
X_ORDER = (2, 1, 3)
ROW_ORDER = ((1, 2), (1, 1), (1, 3), (1, 0), (0, 2), (0, 1), (0, 3))


def split_halves(x):
    high = x.astype(BF)
    return high, (x - high.astype(F32)).astype(BF)


def fine_block(rows, right):
    return lax.dot_general(rows, right, (((0,), (0,)), ((), ())), preferred_element_type=F32).astype(BF)


def remote(src, dst, send_sem, recv_sem, **device):
    return pltpu.make_async_remote_copy(
        src_ref=src, dst_ref=dst, send_sem=send_sem, recv_sem=recv_sem, device_id=device, device_id_type=MESH
    )


def exchange(
    cor_ref, kb_ref, ci_ref, tr_ref, row_ref, fine_ref, right_ref, rows_ref, w_ref,
    cor, kbuf, kt, cbuf, tbuf, ypart, ybuf, pwide, pbuf, zbuf, sbuf, xbuf, fbuf,
    lsem, ksend, krecv, ysend, yrecv, zsend, zrecv, xsend, xrecv, fsend, frecv,
):
    r = lax.axis_index("row")
    c = lax.axis_index("col")
    y, zlo, core = c // 4, lax.rem(c // 2, 2), lax.rem(c, 2)

    load_t = pltpu.make_async_copy(tr_ref, tbuf, lsem.at[0])
    load_c = pltpu.make_async_copy(ci_ref, cbuf, lsem.at[1])
    load_k = pltpu.make_async_copy(kb_ref.at[:, 0], kbuf.at[pl.ds(0, 4)], lsem.at[2])
    load_p = pltpu.make_async_copy(cor_ref, cor, lsem.at[3])
    load_r = pltpu.make_async_copy(row_ref, rows_ref, lsem.at[4])
    load_t.start()
    load_c.start()
    load_k.start()

    col_peers = [
        lax.rem(y + dy, 4) * 4 + lax.rem(zlo + flip, 2) * 2 + lax.rem(core + dc, 2) for dy, flip, dc in COL_ORDER
    ]
    half, x = r // 4, lax.rem(r, 4)
    z_peer = (1 - half) * 4 + x
    x_peers = [lax.rem(x + dx, 4) for dx in X_ORDER]
    barrier = pltpu.get_barrier_semaphore()
    row_peers = [lax.rem(half + dz, 2) * 4 + lax.rem(x + dx, 4) for dz, dx in ROW_ORDER]
    for peer in row_peers:
        pl.semaphore_signal(barrier, inc=1, device_id={"row": peer}, device_id_type=MESH)
    for peer in col_peers:
        pl.semaphore_signal(barrier, inc=1, device_id={"col": peer}, device_id_type=MESH)
    load_p.start()
    load_r.start()

    load_t.wait()
    load_c.wait()
    part = None
    for m in range(MD):
        term = lax.dot_general(tbuf[m], cbuf[m], (((1,), (1,)), ((), ())), preferred_element_type=F32)
        part = term if part is None else part + term
    high, low = split_halves(part)
    both = jnp.concatenate([high.astype(F32), low.astype(F32)], axis=0).astype(BF)
    ypart[...] = both
    ybuf[0, core] = both
    load_k.wait()

    def right_block(p):
        for m in range(MD):
            right_ref[p, :, m * S:(m + 1) * S] = jnp.dot(kbuf[p], cbuf[m], preferred_element_type=F32).astype(BF)

    pl.semaphore_wait(barrier, NCOL + NROW - 2)

    k_copy = remote(kbuf.at[0], kbuf.at[4], ksend, krecv, col=lax.rem(c + NCOL - 1, NCOL))
    y_copies = []
    for i, ((dy, flip, _), peer) in enumerate(zip(COL_ORDER, col_peers)):
        unit = UNITS.index((-dy % 4, flip))
        y_copies.append(remote(ypart, ybuf.at[unit, core], ysend.at[i], yrecv.at[unit, core], col=peer))
    for copy in y_copies:
        copy.start()
    k_copy.start()

    @pl.loop(0, 4)
    def _(p):
        kt[p] = kbuf[p].T
        right_block(p)

    def wait_y(start, stop):
        for unit in range(start, stop):
            for dc in range(2):
                if unit or dc:
                    other = lax.rem(core + dc, 2)
                    remote(ypart, ybuf.at[unit, other], ysend.at[0], yrecv.at[unit, other], col=c).wait_recv()

    def fine_range(start, stop):
        @pl.loop(start, stop, step=2)
        def _(k):
            for i in range(2):
                position = jnp.clip(cor[c * KD + k + i] - c * 4, 0, NB - 1)
                out = fine_block(rows_ref[k + i], right_ref[position])
                for m in range(MD):
                    fine_ref[k + i, m] = out[:, m * S:(m + 1) * S]

    def partial(start, stop, blocks):
        left = ybuf[start:stop].astype(F32).reshape((stop - start) * 16, S).astype(BF)
        n = stop - start
        first = lax.broadcasted_iota(jnp.int32, (n, 8, S), 1) < 4
        for p in blocks:
            both = jnp.dot(left, kt[p], preferred_element_type=F32).reshape(n, 2, 8, S)
            both = both + jnp.concatenate([both[:, :, 4:], both[:, :, :4]], axis=2)
            wide = jnp.where(first, both[:, 0], both[:, 1]).reshape(n * 8, S)
            pwide[p, start * 8:stop * 8] = wide
            pbuf[p, start * 8:stop * 8] = wide.astype(BF)

    near, far = pl.ds(0, NEAR), pl.ds(NEAR, NV - NEAR)
    sent = 2 - 2 * half

    def z_copy(i, src, dst):
        return remote(src, dst, zsend.at[i], zrecv.at[i], row=z_peer)

    z_copies = [
        z_copy(0, pbuf.at[pl.ds(sent, 2), near], zbuf.at[pl.ds(0, 2)]),
        z_copy(1, pbuf.at[sent + 2, near], zbuf.at[2]),
    ]
    far_copies = [
        remote(pbuf.at[pl.ds(peer // 2, 2), far], fbuf.at[r], fsend.at[i], frecv.at[r], row=peer)
        for i, peer in enumerate(row_peers)
    ]

    def add_halves(i):
        sbuf[i] = (pwide[2 * half + i, :NEAR] + zbuf[i].astype(F32)).astype(BF)

    def send_x(place, blocks, dst):
        for i, other in enumerate(x_peers):

            @pl.when(other // 2 == place)
            def _():
                remote(blocks, dst, xsend.at[i], xrecv.at[x], row=half * 4 + other).start()

    load_p.wait()
    load_r.wait()

    wait_y(0, 7)
    partial(0, 7, range(4))
    z_copies[0].start()
    fine_range(CUTS[0], CUTS[1])

    k_copy.wait_recv()
    kt[4] = kbuf[4].T
    partial(0, 7, (4,))
    z_copies[1].start()

    wait_y(7, 8)
    partial(7, 8, range(NB))
    for copy in far_copies:
        copy.start()
    fine_range(CUTS[1], CUTS[2])

    z_copies[0].wait_recv()
    add_halves(0)
    add_halves(1)
    send_x(0, sbuf.at[pl.ds(0, 2)], xbuf.at[x])
    send_x(1, sbuf.at[1], xbuf.at[x, 0])
    z_copies[1].wait_recv()
    add_halves(2)
    send_x(1, sbuf.at[2], xbuf.at[x, 1])

    right_block(4)
    fine_range(CUTS[2], CUTS[3])

    k_copy.wait_send()
    for copy in y_copies:
        copy.wait_send()
    for copy in z_copies:
        copy.wait_send()
    total = sbuf[pl.ds(x // 2, 2)].astype(F32)
    for other in reversed(x_peers):
        remote(xbuf.at[other], xbuf.at[other], xsend.at[0], xrecv.at[other], row=r).wait_recv()
        total += xbuf[other].astype(F32)

    def place(i):
        dy, flip = UNITS[i]
        return lax.rem(y + dy, 4) * 2 + lax.rem(zlo + flip, 2)

    for i in range(7):
        w_ref[:, place(i)] = total[:, i * 8:(i + 1) * 8]
    last = pwide[pl.ds(r // 2, 2), NEAR:]
    for peer in reversed(row_peers):
        remote(fbuf.at[peer], fbuf.at[peer], fsend.at[0], frecv.at[peer], row=r).wait_recv()
        last += fbuf[peer].astype(F32)
    w_ref[:, place(7)] = last
    for i, other in enumerate(x_peers):
        remote(xbuf.at[other], xbuf.at[other], xsend.at[i], xrecv.at[other], row=r).wait_send()
    for copy in far_copies:
        copy.wait_send()


def finish(
    cor_ref, early_ref, right_ref, rows_ref, w_ref, fine_ref, app_ref, cor, late, app, wsplit, sem, esem, lsem, asem
):
    r = lax.axis_index("row")
    c = lax.axis_index("col")
    load_p = pltpu.make_async_copy(cor_ref, cor, sem)
    load_p.start()
    early = [
        pltpu.make_async_copy(early_ref.at[pl.ds(i * 4, 4)], fine_ref.at[pl.ds(i * 4, 4)], esem.at[i])
        for i in range(EARLY // 4)
    ]
    for copy in early:
        copy.start()
    for i in range(2):
        high, low = split_halves(w_ref[i].reshape(NV, S))
        wsplit[i, :NV] = high
        wsplit[i, NV:] = low
    load_p.wait()

    def position_of(k):
        return jnp.clip(cor[c * KD + k] - c * 4, 0, NB - 1)

    def late_copy(k):
        return pltpu.make_async_copy(late.at[pl.ds(k, 2)], fine_ref.at[pl.ds(EARLY + k, 2)], lsem.at[k // 2])

    @pl.loop(0, KD - EARLY, step=2)
    def _(k):
        for i in range(2):
            out = fine_block(rows_ref[EARLY + k + i], right_ref[position_of(EARLY + k + i)])
            for m in range(MD):
                late[k + i, m] = out[:, m * S:(m + 1) * S]
        late_copy(k).start()

    for i in range(4):
        k = r * 4 + i
        which = jnp.clip(position_of(k) - r // 2, 0, 1)
        x = jnp.dot(wsplit[which], rows_ref[k], preferred_element_type=F32)
        app[i] = (x[:NV] + x[NV:]).astype(BF)
    app_copy = pltpu.make_async_copy(app, app_ref, asem)
    app_copy.start()

    for copy in early:
        copy.wait()

    @pl.loop(0, KD - EARLY, step=2)
    def _(k):
        late_copy(k).wait()

    app_copy.wait()


def per_device(kernel_blocks, row_intersection, col_intersection, trial, coarse_of_row):
    hbm_spec = pl.BlockSpec(memory_space=pltpu.HBM)
    vmem_spec = pl.BlockSpec(memory_space=pltpu.VMEM)
    arrays = (coarse_of_row, kernel_blocks, col_intersection, trial, row_intersection)
    arrays = [pltpu.with_memory_space_constraint(x, pltpu.HBM) for x in arrays]
    early, right, rows, w = pl.pallas_call(
        exchange,
        out_shape=(
            jax.ShapeDtypeStruct((EARLY, MD, S, S), BF),
            jax.ShapeDtypeStruct((NB, S, MD * S), BF),
            jax.ShapeDtypeStruct((KD, S, S), BF),
            jax.ShapeDtypeStruct((2, 8, 8, S), F32),
        ),
        in_specs=[hbm_spec] * 5,
        out_specs=(vmem_spec,) * 4,
        scratch_shapes=[
            pltpu.SMEM((NCOL * KD,), jnp.int32),
            pltpu.VMEM((NB, S, S), BF),
            pltpu.VMEM((NB, S, S), BF),
            pltpu.VMEM((MD, S, S), BF),
            pltpu.VMEM((MD, 4, S), BF),
            pltpu.VMEM((8, S), BF),
            pltpu.VMEM((8, 2, 8, S), BF),
            pltpu.VMEM((NB, NV, S), F32),
            pltpu.VMEM((NB, NV, S), BF),
            pltpu.VMEM((3, NEAR, S), BF),
            pltpu.VMEM((3, NEAR, S), BF),
            pltpu.VMEM((4, 2, NEAR, S), BF),
            pltpu.VMEM((NROW, 2, NV - NEAR, S), BF),
            pltpu.SemaphoreType.DMA((5,)),
            pltpu.SemaphoreType.DMA,
            pltpu.SemaphoreType.DMA,
            pltpu.SemaphoreType.DMA((NCOL,)),
            pltpu.SemaphoreType.DMA((8, 2)),
            pltpu.SemaphoreType.DMA((2,)),
            pltpu.SemaphoreType.DMA((2,)),
            pltpu.SemaphoreType.DMA((3,)),
            pltpu.SemaphoreType.DMA((4,)),
            pltpu.SemaphoreType.DMA((NROW,)),
            pltpu.SemaphoreType.DMA((NROW,)),
        ],
        compiler_params=pltpu.CompilerParams(
            collective_id=0, has_side_effects=True, vmem_limit_bytes=28 << 20
        ),
        name="exchange",
    )(*arrays)

    return pl.pallas_call(
        finish,
        out_shape=(jax.ShapeDtypeStruct((KD, MD, S, S), BF), jax.ShapeDtypeStruct((4, NV, S), BF)),
        in_specs=[hbm_spec] + [vmem_spec] * 4,
        out_specs=(hbm_spec, hbm_spec),
        scratch_shapes=[
            pltpu.SMEM((NCOL * KD,), jnp.int32),
            pltpu.VMEM((KD - EARLY, MD, S, S), BF),
            pltpu.VMEM((4, NV, S), BF),
            pltpu.VMEM((2, 2 * NV, S), BF),
            pltpu.SemaphoreType.DMA,
            pltpu.SemaphoreType.DMA((EARLY // 4,)),
            pltpu.SemaphoreType.DMA(((KD - EARLY) // 2,)),
            pltpu.SemaphoreType.DMA,
        ],
        compiler_params=pltpu.CompilerParams(vmem_limit_bytes=28 << 20),
        name="finish",
    )(arrays[0], early, right, rows, w)


def solution(mesh):
    in_specs = (
        P("col", "row", None, None),
        P("col", None, None),
        P("row", None, None),
        P("row", "col", None),
        P(),
    )
    out_specs = (P("col", "row", None, None), P(("col", "row"), None, None))
    return jax.shard_map(
        per_device, mesh=mesh, in_specs=in_specs, out_specs=out_specs, check_vma=False
    )
```

```python
import jax
import jax.numpy as jnp
from jax import lax
from jax.experimental import pallas as pl
from jax.experimental.pallas import tpu as pltpu
from jax.sharding import PartitionSpec as P

MESH = pl.DeviceIdType.MESH
BF = jnp.bfloat16
F32 = jnp.float32
NROW, NCOL = 8, 16
S = 256
NV = 64
KD = 32
MD = 4
NB = 5
CUTS = (0, 2, 4, 6, 16)
EARLY = CUTS[-1]
FIRST = 12
BEGUN = 4
NEAR = 56
PARTS = ((0, 3), (3, 5), (5, 7))
UNITS = ((0, 0), (3, 0), (1, 0), (0, 1), (2, 0), (3, 1), (1, 1), (2, 1))
COL_ORDER = [
    (dy, flip, dc)
    for dy, flip in ((2, 1), (1, 1), (3, 1), (2, 0), (0, 1), (1, 0), (3, 0), (0, 0))
    for dc in range(2)
    if dy or flip or dc
]
X_ORDER = (2, 1, 3)
ROW_ORDER = ((1, 2), (1, 1), (1, 3), (1, 0), (0, 2), (0, 1), (0, 3))


def split_halves(x):
    high = x.astype(BF)
    return high, (x - high.astype(F32)).astype(BF)


def fine_block(rows, right):
    return lax.dot_general(rows, right, (((0,), (0,)), ((), ())), preferred_element_type=F32).astype(BF)


def remote(src, dst, send_sem, recv_sem, **device):
    return pltpu.make_async_remote_copy(
        src_ref=src, dst_ref=dst, send_sem=send_sem, recv_sem=recv_sem, device_id=device, device_id_type=MESH
    )


def first_count(r, c):
    return jnp.where((r == 0) & (c < 2), BEGUN, 0)


def store_block(ref, k, rows, right):
    out = fine_block(rows, right)
    for m in range(MD):
        ref[k, m] = out[:, m * S:(m + 1) * S]


def begin(cor_ref, kb_ref, ci_ref, row_ref, fine_ref, token_ref, cor, kbuf, cbuf, rows, right, blocks, lsem, wsem):
    c = lax.axis_index("col")
    count = first_count(lax.axis_index("row"), c)
    token_ref[...] = jnp.zeros_like(token_ref)

    @pl.when(count > 0)
    def _():
        load_k = pltpu.make_async_copy(kb_ref.at[pl.ds(0, 2), 0], kbuf, lsem.at[0])
        load_c = pltpu.make_async_copy(ci_ref, cbuf, lsem.at[1])
        load_p = pltpu.make_async_copy(cor_ref, cor, lsem.at[2])
        load_r = pltpu.make_async_copy(row_ref.at[pl.ds(0, BEGUN)], rows, lsem.at[3])
        for copy in (load_k, load_c, load_p, load_r):
            copy.start()
        load_k.wait()
        load_c.wait()

        @pl.loop(0, 2)
        def _(p):
            for m in range(MD):
                right[p, :, m * S:(m + 1) * S] = jnp.dot(kbuf[p], cbuf[m], preferred_element_type=F32).astype(BF)

        load_p.wait()
        load_r.wait()

        def block_copy(k):
            return pltpu.make_async_copy(blocks.at[pl.ds(k, 2)], fine_ref.at[pl.ds(k, 2)], wsem.at[k // 2])

        @pl.loop(0, BEGUN, step=2)
        def _(k):
            for i in range(2):
                position = jnp.clip(cor[c * KD + k + i] - c * 4, 0, 1)
                store_block(blocks, k + i, rows[k + i], right[position])
            block_copy(k).start()

        @pl.loop(0, BEGUN, step=2)
        def _(k):
            block_copy(k).wait()


def exchange(
    token_ref, cor_ref, kb_ref, ci_ref, tr_ref, row_ref, fine_ref, right_ref, rows_ref, w_ref,
    cor, kbuf, kt, cbuf, tbuf, ypart, ybuf, pwide, pbuf, zbuf, sbuf, xbuf, fbuf,
    lsem, ksend, krecv, ysend, yrecv, zsend, zrecv, xsend, xrecv, fsend, frecv,
):
    r = lax.axis_index("row")
    c = lax.axis_index("col")
    y, zlo, core = c // 4, lax.rem(c // 2, 2), lax.rem(c, 2)

    load_t = pltpu.make_async_copy(tr_ref, tbuf, lsem.at[0])
    load_c = pltpu.make_async_copy(ci_ref, cbuf, lsem.at[1])
    load_k = pltpu.make_async_copy(kb_ref.at[:, 0], kbuf.at[pl.ds(0, 4)], lsem.at[2])
    load_p = pltpu.make_async_copy(cor_ref, cor, lsem.at[3])
    load_r = pltpu.make_async_copy(row_ref, rows_ref, lsem.at[4])
    load_t.start()
    load_c.start()
    load_k.start()

    col_peers = [
        lax.rem(y + dy, 4) * 4 + lax.rem(zlo + flip, 2) * 2 + lax.rem(core + dc, 2) for dy, flip, dc in COL_ORDER
    ]
    half, x = r // 4, lax.rem(r, 4)
    z_peer = (1 - half) * 4 + x
    x_peers = [lax.rem(x + dx, 4) for dx in X_ORDER]
    barrier = pltpu.get_barrier_semaphore()
    row_peers = [lax.rem(half + dz, 2) * 4 + lax.rem(x + dx, 4) for dz, dx in ROW_ORDER]
    for peer in row_peers:
        pl.semaphore_signal(barrier, inc=1, device_id={"row": peer}, device_id_type=MESH)
    for peer in col_peers:
        pl.semaphore_signal(barrier, inc=1, device_id={"col": peer}, device_id_type=MESH)
    load_p.start()
    load_r.start()

    load_t.wait()
    load_c.wait()
    part = None
    for m in range(MD):
        term = lax.dot_general(tbuf[m], cbuf[m], (((1,), (1,)), ((), ())), preferred_element_type=F32)
        part = term if part is None else part + term
    high, low = split_halves(part)
    both = jnp.concatenate([high.astype(F32), low.astype(F32)], axis=0).astype(BF)
    ypart[...] = both
    ybuf[0, core] = both
    load_k.wait()

    def right_block(p):
        for m in range(MD):
            right_ref[p, :, m * S:(m + 1) * S] = jnp.dot(kbuf[p], cbuf[m], preferred_element_type=F32).astype(BF)

    pl.semaphore_wait(barrier, NCOL + NROW - 2)

    k_copy = remote(kbuf.at[0], kbuf.at[4], ksend, krecv, col=lax.rem(c + NCOL - 1, NCOL))
    y_copies = []
    for i, ((dy, flip, _), peer) in enumerate(zip(COL_ORDER, col_peers)):
        unit = UNITS.index((-dy % 4, flip))
        y_copies.append(remote(ypart, ybuf.at[unit, core], ysend.at[i], yrecv.at[unit, core], col=peer))
    for copy in y_copies:
        copy.start()
    k_copy.start()

    @pl.loop(0, 4)
    def _(p):
        kt[p] = kbuf[p].T
        right_block(p)

    def wait_y(start, stop):
        for unit in range(start, stop):
            for dc in range(2):
                if unit or dc:
                    other = lax.rem(core + dc, 2)
                    remote(ypart, ybuf.at[unit, other], ysend.at[0], yrecv.at[unit, other], col=c).wait_recv()

    def fine_range(start, stop):
        @pl.loop(start, stop, step=2)
        def _(k):
            for i in range(2):
                position = jnp.clip(cor[c * KD + FIRST + k + i] - c * 4, 0, NB - 1)
                store_block(fine_ref, k + i, rows_ref[FIRST + k + i], right_ref[position])

    def partial(start, stop, blocks):
        left = ybuf[start:stop].astype(F32).reshape((stop - start) * 16, S).astype(BF)
        n = stop - start
        first = lax.broadcasted_iota(jnp.int32, (n, 8, S), 1) < 4
        for p in blocks:
            both = jnp.dot(left, kt[p], preferred_element_type=F32).reshape(n, 2, 8, S)
            both = both + jnp.concatenate([both[:, :, 4:], both[:, :, :4]], axis=2)
            wide = jnp.where(first, both[:, 0], both[:, 1]).reshape(n * 8, S)
            pwide[p, start * 8:stop * 8] = wide
            pbuf[p, start * 8:stop * 8] = wide.astype(BF)

    near, far = pl.ds(0, NEAR), pl.ds(NEAR, NV - NEAR)
    sent = 2 - 2 * half

    def z_copy(i, src, dst):
        return remote(src, dst, zsend.at[i], zrecv.at[i], row=z_peer)

    z_copies = [
        z_copy(i, pbuf.at[pl.ds(sent, 2), rows], zbuf.at[pl.ds(0, 2), rows])
        for i, rows in enumerate(pl.ds(a * 8, (b - a) * 8) for a, b in PARTS)
    ]
    z_copies.append(z_copy(len(PARTS), pbuf.at[sent + 2, near], zbuf.at[2]))
    far_copies = [
        remote(pbuf.at[pl.ds(peer // 2, 2), far], fbuf.at[r], fsend.at[i], frecv.at[r], row=peer)
        for i, peer in enumerate(row_peers)
    ]

    def add_halves(i, start, stop):
        sbuf[i, start:stop] = (pwide[2 * half + i, start:stop] + zbuf[i, start:stop].astype(F32)).astype(BF)

    def send_x(place, blocks, dst):
        for i, other in enumerate(x_peers):

            @pl.when(other // 2 == place)
            def _():
                remote(blocks, dst, xsend.at[i], xrecv.at[x], row=half * 4 + other).start()

    load_p.wait()
    load_r.wait()

    for i, (a, b) in enumerate(PARTS):
        wait_y(a, b)
        partial(a, b, range(4))
        z_copies[i].start()
    fine_range(CUTS[0], CUTS[1])

    k_copy.wait_recv()
    kt[4] = kbuf[4].T
    partial(0, 7, (4,))
    z_copies[-1].start()

    wait_y(7, 8)
    partial(7, 8, range(NB))
    for copy in far_copies:
        copy.start()
    fine_range(CUTS[1], CUTS[2])

    for i, (a, b) in enumerate(PARTS):
        z_copies[i].wait_recv()
        add_halves(0, a * 8, b * 8)
        add_halves(1, a * 8, b * 8)
        rows = pl.ds(a * 8, (b - a) * 8)
        send_x(0, sbuf.at[pl.ds(0, 2), rows], xbuf.at[x, :, rows])
        send_x(1, sbuf.at[1, rows], xbuf.at[x, 0, rows])
        if i == 0:
            fine_range(CUTS[2], CUTS[3])
    z_copies[-1].wait_recv()
    add_halves(2, 0, NEAR)
    send_x(1, sbuf.at[2], xbuf.at[x, 1])

    right_block(4)
    fine_range(CUTS[3], CUTS[4])

    k_copy.wait_send()
    for copy in y_copies:
        copy.wait_send()
    for copy in z_copies:
        copy.wait_send()
    total = sbuf[pl.ds(x // 2, 2)].astype(F32)
    for other in reversed(x_peers):
        remote(xbuf.at[other], xbuf.at[other], xsend.at[0], xrecv.at[other], row=r).wait_recv()
        total += xbuf[other].astype(F32)

    def place(i):
        dy, flip = UNITS[i]
        return lax.rem(y + dy, 4) * 2 + lax.rem(zlo + flip, 2)

    for i in range(7):
        w_ref[:, place(i)] = total[:, i * 8:(i + 1) * 8]
    last = pwide[pl.ds(r // 2, 2), NEAR:]
    for peer in reversed(row_peers):
        remote(fbuf.at[peer], fbuf.at[peer], fsend.at[0], frecv.at[peer], row=r).wait_recv()
        last += fbuf[peer].astype(F32)
    w_ref[:, place(7)] = last
    for i, other in enumerate(x_peers):
        remote(xbuf.at[other], xbuf.at[other], xsend.at[i], xrecv.at[other], row=r).wait_send()
    for copy in far_copies:
        copy.wait_send()


def finish(
    cor_ref, early_ref, right_ref, rows_ref, w_ref, begun_ref, fine_ref, app_ref,
    cor, late, app, wsplit, sem, esem, lsem, asem,
):
    r = lax.axis_index("row")
    c = lax.axis_index("col")
    load_p = pltpu.make_async_copy(cor_ref, cor, sem)
    load_p.start()
    early = [
        pltpu.make_async_copy(early_ref.at[pl.ds(i * 4, 4)], fine_ref.at[pl.ds(FIRST + i * 4, 4)], esem.at[i])
        for i in range(EARLY // 4)
    ]
    for copy in early:
        copy.start()
    for i in range(2):
        high, low = split_halves(w_ref[i].reshape(NV, S))
        wsplit[i, :NV] = high
        wsplit[i, NV:] = low
    load_p.wait()
    count = first_count(r, c)

    def position_of(k):
        return jnp.clip(cor[c * KD + k] - c * 4, 0, NB - 1)

    def late_copy(slot):
        k = slot + jnp.where(slot < FIRST, 0, EARLY)
        return pltpu.make_async_copy(late.at[pl.ds(slot, 2)], fine_ref.at[pl.ds(k, 2)], lsem.at[slot // 2])

    @pl.loop(count, KD - EARLY, step=2)
    def _(slot):
        for i in range(2):
            k = slot + i + jnp.where(slot < FIRST, 0, EARLY)
            store_block(late, slot + i, rows_ref[k], right_ref[position_of(k)])
        late_copy(slot).start()

    for i in range(4):
        k = r * 4 + i
        which = jnp.clip(position_of(k) - r // 2, 0, 1)
        x = jnp.dot(wsplit[which], rows_ref[k], preferred_element_type=F32)
        app[i] = (x[:NV] + x[NV:]).astype(BF)
    app_copy = pltpu.make_async_copy(app, app_ref, asem)
    app_copy.start()

    for copy in early:
        copy.wait()

    @pl.loop(count, KD - EARLY, step=2)
    def _(slot):
        late_copy(slot).wait()

    app_copy.wait()


def per_device(kernel_blocks, row_intersection, col_intersection, trial, coarse_of_row):
    hbm_spec = pl.BlockSpec(memory_space=pltpu.HBM)
    vmem_spec = pl.BlockSpec(memory_space=pltpu.VMEM)
    arrays = (coarse_of_row, kernel_blocks, col_intersection, trial, row_intersection)
    arrays = [pltpu.with_memory_space_constraint(x, pltpu.HBM) for x in arrays]
    begun, token = pl.pallas_call(
        begin,
        out_shape=(jax.ShapeDtypeStruct((KD, MD, S, S), BF), jax.ShapeDtypeStruct((8, 128), F32)),
        in_specs=[hbm_spec] * 4,
        out_specs=(hbm_spec, vmem_spec),
        scratch_shapes=[
            pltpu.SMEM((NCOL * KD,), jnp.int32),
            pltpu.VMEM((2, S, S), BF),
            pltpu.VMEM((MD, S, S), BF),
            pltpu.VMEM((BEGUN, S, S), BF),
            pltpu.VMEM((2, S, MD * S), BF),
            pltpu.VMEM((BEGUN, MD, S, S), BF),
            pltpu.SemaphoreType.DMA((4,)),
            pltpu.SemaphoreType.DMA((BEGUN // 2,)),
        ],
        compiler_params=pltpu.CompilerParams(vmem_limit_bytes=28 << 20),
        name="begin",
    )(arrays[0], arrays[1], arrays[2], arrays[4])
    early, right, rows, w = pl.pallas_call(
        exchange,
        out_shape=(
            jax.ShapeDtypeStruct((EARLY, MD, S, S), BF),
            jax.ShapeDtypeStruct((NB, S, MD * S), BF),
            jax.ShapeDtypeStruct((KD, S, S), BF),
            jax.ShapeDtypeStruct((2, 8, 8, S), F32),
        ),
        in_specs=[pl.BlockSpec(memory_space=pl.ANY)] + [hbm_spec] * 5,
        out_specs=(vmem_spec,) * 4,
        scratch_shapes=[
            pltpu.SMEM((NCOL * KD,), jnp.int32),
            pltpu.VMEM((NB, S, S), BF),
            pltpu.VMEM((NB, S, S), BF),
            pltpu.VMEM((MD, S, S), BF),
            pltpu.VMEM((MD, 4, S), BF),
            pltpu.VMEM((8, S), BF),
            pltpu.VMEM((8, 2, 8, S), BF),
            pltpu.VMEM((NB, NV, S), F32),
            pltpu.VMEM((NB, NV, S), BF),
            pltpu.VMEM((3, NEAR, S), BF),
            pltpu.VMEM((3, NEAR, S), BF),
            pltpu.VMEM((4, 2, NEAR, S), BF),
            pltpu.VMEM((NROW, 2, NV - NEAR, S), BF),
            pltpu.SemaphoreType.DMA((5,)),
            pltpu.SemaphoreType.DMA,
            pltpu.SemaphoreType.DMA,
            pltpu.SemaphoreType.DMA((NCOL,)),
            pltpu.SemaphoreType.DMA((8, 2)),
            pltpu.SemaphoreType.DMA((len(PARTS) + 1,)),
            pltpu.SemaphoreType.DMA((len(PARTS) + 1,)),
            pltpu.SemaphoreType.DMA((3,)),
            pltpu.SemaphoreType.DMA((4,)),
            pltpu.SemaphoreType.DMA((NROW,)),
            pltpu.SemaphoreType.DMA((NROW,)),
        ],
        compiler_params=pltpu.CompilerParams(
            collective_id=0, has_side_effects=True, vmem_limit_bytes=28 << 20
        ),
        name="exchange",
    )(token, *arrays)

    return pl.pallas_call(
        finish,
        out_shape=(jax.ShapeDtypeStruct((KD, MD, S, S), BF), jax.ShapeDtypeStruct((4, NV, S), BF)),
        in_specs=[hbm_spec] + [vmem_spec] * 4 + [hbm_spec],
        out_specs=(hbm_spec, hbm_spec),
        scratch_shapes=[
            pltpu.SMEM((NCOL * KD,), jnp.int32),
            pltpu.VMEM((KD - EARLY, MD, S, S), BF),
            pltpu.VMEM((4, NV, S), BF),
            pltpu.VMEM((2, 2 * NV, S), BF),
            pltpu.SemaphoreType.DMA,
            pltpu.SemaphoreType.DMA((EARLY // 4,)),
            pltpu.SemaphoreType.DMA(((KD - EARLY) // 2,)),
            pltpu.SemaphoreType.DMA,
        ],
        compiler_params=pltpu.CompilerParams(vmem_limit_bytes=28 << 20),
        input_output_aliases={5: 0},
        name="finish",
    )(arrays[0], early, right, rows, w, begun)


def solution(mesh):
    in_specs = (
        P("col", "row", None, None),
        P("col", None, None),
        P("row", None, None),
        P("row", "col", None),
        P(),
    )
    out_specs = (P("col", "row", None, None), P(("col", "row"), None, None))
    return jax.shard_map(
        per_device, mesh=mesh, in_specs=in_specs, out_specs=out_specs, check_vma=False
    )
```

```python
import jax
import jax.numpy as jnp
from jax import lax
from jax.experimental import pallas as pl
from jax.experimental.pallas import tpu as pltpu
from jax.sharding import PartitionSpec as P

MESH = pl.DeviceIdType.MESH
BF = jnp.bfloat16
F32 = jnp.float32
NROW, NCOL = 8, 16
S = 256
NV = 64
KD = 32
MD = 4
NB = 5
CUTS = (0, 2, 6, 6, 14)
EARLY = CUTS[-1]
FIRST = 12
BEGUN = 4
NEAR = 56
PARTS = ((0, 3), (3, 5), (5, 7))
UNITS = ((0, 0), (3, 0), (1, 0), (0, 1), (2, 0), (3, 1), (1, 1), (2, 1))
COL_ORDER = [
    (dy, flip, dc)
    for dy, flip in ((2, 1), (1, 1), (3, 1), (2, 0), (0, 1), (1, 0), (3, 0), (0, 0))
    for dc in range(2)
    if dy or flip or dc
]
X_ORDER = (2, 1, 3)
ROW_ORDER = ((1, 2), (1, 1), (1, 3), (1, 0), (0, 2), (0, 1), (0, 3))


def split_halves(x):
    high = x.astype(BF)
    return high, (x - high.astype(F32)).astype(BF)


def fine_block(rows, right):
    return lax.dot_general(rows, right, (((0,), (0,)), ((), ())), preferred_element_type=F32).astype(BF)


def remote(src, dst, send_sem, recv_sem, **device):
    return pltpu.make_async_remote_copy(
        src_ref=src, dst_ref=dst, send_sem=send_sem, recv_sem=recv_sem, device_id=device, device_id_type=MESH
    )


def first_count(r, c):
    return jnp.where((r == 0) & (c < 2), BEGUN, 0)


def store_block(ref, k, rows, right):
    out = fine_block(rows, right)
    for m in range(MD):
        ref[k, m] = out[:, m * S:(m + 1) * S]


def begin(cor_ref, kb_ref, ci_ref, row_ref, fine_ref, token_ref, cor, kbuf, cbuf, rows, right, blocks, lsem, wsem):
    c = lax.axis_index("col")
    count = first_count(lax.axis_index("row"), c)
    token_ref[...] = jnp.zeros_like(token_ref)

    @pl.when(count > 0)
    def _():
        load_k = pltpu.make_async_copy(kb_ref.at[pl.ds(0, 2), 0], kbuf, lsem.at[0])
        load_c = pltpu.make_async_copy(ci_ref, cbuf, lsem.at[1])
        load_p = pltpu.make_async_copy(cor_ref, cor, lsem.at[2])
        load_r = pltpu.make_async_copy(row_ref.at[pl.ds(0, BEGUN)], rows, lsem.at[3])
        for copy in (load_k, load_c, load_p, load_r):
            copy.start()
        load_k.wait()
        load_c.wait()

        @pl.loop(0, 2)
        def _(p):
            for m in range(MD):
                right[p, :, m * S:(m + 1) * S] = jnp.dot(kbuf[p], cbuf[m], preferred_element_type=F32).astype(BF)

        load_p.wait()
        load_r.wait()

        def block_copy(k):
            return pltpu.make_async_copy(blocks.at[pl.ds(k, 2)], fine_ref.at[pl.ds(k, 2)], wsem.at[k // 2])

        @pl.loop(0, BEGUN, step=2)
        def _(k):
            for i in range(2):
                position = jnp.clip(cor[c * KD + k + i] - c * 4, 0, 1)
                store_block(blocks, k + i, rows[k + i], right[position])
            block_copy(k).start()

        @pl.loop(0, BEGUN, step=2)
        def _(k):
            block_copy(k).wait()


def exchange(
    token_ref, cor_ref, kb_ref, ci_ref, tr_ref, row_ref, fine_ref, right_ref, rows_ref, w_ref,
    cor, kbuf, kt, cbuf, tbuf, ypart, ybuf, pwide, pbuf, zbuf, sbuf, xbuf, fbuf,
    lsem, ksend, krecv, ysend, yrecv, zsend, zrecv, xsend, xrecv, fsend, frecv,
):
    r = lax.axis_index("row")
    c = lax.axis_index("col")
    y, zlo, core = c // 4, lax.rem(c // 2, 2), lax.rem(c, 2)

    load_t = pltpu.make_async_copy(tr_ref, tbuf, lsem.at[0])
    load_c = pltpu.make_async_copy(ci_ref, cbuf, lsem.at[1])
    load_k = pltpu.make_async_copy(kb_ref.at[:, 0], kbuf.at[pl.ds(0, 4)], lsem.at[2])
    load_p = pltpu.make_async_copy(cor_ref, cor, lsem.at[3])
    load_r = pltpu.make_async_copy(row_ref, rows_ref, lsem.at[4])
    load_t.start()
    load_c.start()
    load_k.start()

    col_peers = [
        lax.rem(y + dy, 4) * 4 + lax.rem(zlo + flip, 2) * 2 + lax.rem(core + dc, 2) for dy, flip, dc in COL_ORDER
    ]
    half, x = r // 4, lax.rem(r, 4)
    z_peer = (1 - half) * 4 + x
    x_peers = [lax.rem(x + dx, 4) for dx in X_ORDER]
    barrier = pltpu.get_barrier_semaphore()
    row_peers = [lax.rem(half + dz, 2) * 4 + lax.rem(x + dx, 4) for dz, dx in ROW_ORDER]
    for peer in row_peers:
        pl.semaphore_signal(barrier, inc=1, device_id={"row": peer}, device_id_type=MESH)
    for peer in col_peers:
        pl.semaphore_signal(barrier, inc=1, device_id={"col": peer}, device_id_type=MESH)
    load_p.start()
    load_r.start()

    load_t.wait()
    load_c.wait()
    part = None
    for m in range(MD):
        term = lax.dot_general(tbuf[m], cbuf[m], (((1,), (1,)), ((), ())), preferred_element_type=F32)
        part = term if part is None else part + term
    high, low = split_halves(part)
    both = jnp.concatenate([high.astype(F32), low.astype(F32)], axis=0).astype(BF)
    ypart[...] = both
    ybuf[0, core] = both
    load_k.wait()

    def right_block(p):
        for m in range(MD):
            right_ref[p, :, m * S:(m + 1) * S] = jnp.dot(kbuf[p], cbuf[m], preferred_element_type=F32).astype(BF)

    pl.semaphore_wait(barrier, NCOL + NROW - 2)

    k_copy = remote(kbuf.at[0], kbuf.at[4], ksend, krecv, col=lax.rem(c + NCOL - 1, NCOL))
    y_copies = []
    for i, ((dy, flip, _), peer) in enumerate(zip(COL_ORDER, col_peers)):
        unit = UNITS.index((-dy % 4, flip))
        y_copies.append(remote(ypart, ybuf.at[unit, core], ysend.at[i], yrecv.at[unit, core], col=peer))
    for copy in y_copies:
        copy.start()
    k_copy.start()

    @pl.loop(0, 4)
    def _(p):
        kt[p] = kbuf[p].T
        right_block(p)

    def wait_y(start, stop):
        for unit in range(start, stop):
            for dc in range(2):
                if unit or dc:
                    other = lax.rem(core + dc, 2)
                    remote(ypart, ybuf.at[unit, other], ysend.at[0], yrecv.at[unit, other], col=c).wait_recv()

    def fine_range(start, stop):
        @pl.loop(start, stop, step=2)
        def _(k):
            for i in range(2):
                position = jnp.clip(cor[c * KD + FIRST + k + i] - c * 4, 0, NB - 1)
                store_block(fine_ref, k + i, rows_ref[FIRST + k + i], right_ref[position])

    def partial(start, stop, blocks):
        left = ybuf[start:stop].astype(F32).reshape((stop - start) * 16, S).astype(BF)
        n = stop - start
        first = lax.broadcasted_iota(jnp.int32, (n, 8, S), 1) < 4
        for p in blocks:
            both = jnp.dot(left, kt[p], preferred_element_type=F32).reshape(n, 2, 8, S)
            both = both + jnp.concatenate([both[:, :, 4:], both[:, :, :4]], axis=2)
            wide = jnp.where(first, both[:, 0], both[:, 1]).reshape(n * 8, S)
            pwide[p, start * 8:stop * 8] = wide
            pbuf[p, start * 8:stop * 8] = wide.astype(BF)

    near, far = pl.ds(0, NEAR), pl.ds(NEAR, NV - NEAR)
    sent = 2 - 2 * half

    def z_copy(i, src, dst):
        return remote(src, dst, zsend.at[i], zrecv.at[i], row=z_peer)

    z_copies = [
        z_copy(i, pbuf.at[pl.ds(sent, 2), rows], zbuf.at[pl.ds(0, 2), rows])
        for i, rows in enumerate(pl.ds(a * 8, (b - a) * 8) for a, b in PARTS)
    ]
    z_copies.append(z_copy(len(PARTS), pbuf.at[sent + 2, near], zbuf.at[2]))
    far_copies = [
        remote(pbuf.at[pl.ds(peer // 2, 2), far], fbuf.at[r], fsend.at[i], frecv.at[r], row=peer)
        for i, peer in enumerate(row_peers)
    ]

    def add_halves(i, start, stop):
        sbuf[i, start:stop] = (pwide[2 * half + i, start:stop] + zbuf[i, start:stop].astype(F32)).astype(BF)

    def send_x(place, blocks, dst):
        for i, other in enumerate(x_peers):

            @pl.when(other // 2 == place)
            def _():
                remote(blocks, dst, xsend.at[i], xrecv.at[x], row=half * 4 + other).start()

    load_p.wait()
    load_r.wait()

    for i, (a, b) in enumerate(PARTS):
        wait_y(a, b)
        partial(a, b, range(4))
        z_copies[i].start()
    fine_range(CUTS[0], CUTS[1])

    k_copy.wait_recv()
    kt[4] = kbuf[4].T
    partial(0, 7, (4,))
    z_copies[-1].start()

    wait_y(7, 8)
    partial(7, 8, range(NB))
    for copy in far_copies:
        copy.start()
    fine_range(CUTS[1], CUTS[2])

    for i, (a, b) in enumerate(PARTS):
        z_copies[i].wait_recv()
        add_halves(0, a * 8, b * 8)
        add_halves(1, a * 8, b * 8)
        rows = pl.ds(a * 8, (b - a) * 8)
        send_x(0, sbuf.at[pl.ds(0, 2), rows], xbuf.at[x, :, rows])
        send_x(1, sbuf.at[1, rows], xbuf.at[x, 0, rows])
        if i == 0:
            fine_range(CUTS[2], CUTS[3])
    z_copies[-1].wait_recv()
    add_halves(2, 0, NEAR)
    send_x(1, sbuf.at[2], xbuf.at[x, 1])

    right_block(4)
    fine_range(CUTS[3], CUTS[4])

    k_copy.wait_send()
    for copy in y_copies:
        copy.wait_send()
    for copy in z_copies:
        copy.wait_send()
    total = sbuf[pl.ds(x // 2, 2)].astype(F32)
    for other in reversed(x_peers):
        remote(xbuf.at[other], xbuf.at[other], xsend.at[0], xrecv.at[other], row=r).wait_recv()
        total += xbuf[other].astype(F32)

    def place(i):
        dy, flip = UNITS[i]
        return lax.rem(y + dy, 4) * 2 + lax.rem(zlo + flip, 2)

    for i in range(7):
        w_ref[:, place(i)] = total[:, i * 8:(i + 1) * 8]
    last = pwide[pl.ds(r // 2, 2), NEAR:]
    for peer in reversed(row_peers):
        remote(fbuf.at[peer], fbuf.at[peer], fsend.at[0], frecv.at[peer], row=r).wait_recv()
        last += fbuf[peer].astype(F32)
    w_ref[:, place(7)] = last
    for i, other in enumerate(x_peers):
        remote(xbuf.at[other], xbuf.at[other], xsend.at[i], xrecv.at[other], row=r).wait_send()
    for copy in far_copies:
        copy.wait_send()


def finish(
    cor_ref, early_ref, right_ref, rows_ref, w_ref, begun_ref, fine_ref, app_ref,
    cor, late, app, wsplit, sem, esem, lsem, asem,
):
    r = lax.axis_index("row")
    c = lax.axis_index("col")
    load_p = pltpu.make_async_copy(cor_ref, cor, sem)
    load_p.start()
    early = [
        pltpu.make_async_copy(early_ref.at[pl.ds(i * 2, 2)], fine_ref.at[pl.ds(FIRST + i * 2, 2)], esem.at[i])
        for i in range(EARLY // 2)
    ]
    for copy in early:
        copy.start()
    for i in range(2):
        high, low = split_halves(w_ref[i].reshape(NV, S))
        wsplit[i, :NV] = high
        wsplit[i, NV:] = low
    load_p.wait()
    count = first_count(r, c)

    def position_of(k):
        return jnp.clip(cor[c * KD + k] - c * 4, 0, NB - 1)

    def late_copy(slot):
        k = slot + jnp.where(slot < FIRST, 0, EARLY)
        return pltpu.make_async_copy(late.at[pl.ds(slot, 2)], fine_ref.at[pl.ds(k, 2)], lsem.at[slot // 2])

    @pl.loop(count, KD - EARLY, step=2)
    def _(slot):
        for i in range(2):
            k = slot + i + jnp.where(slot < FIRST, 0, EARLY)
            store_block(late, slot + i, rows_ref[k], right_ref[position_of(k)])
        late_copy(slot).start()

    for i in range(4):
        k = r * 4 + i
        which = jnp.clip(position_of(k) - r // 2, 0, 1)
        x = jnp.dot(wsplit[which], rows_ref[k], preferred_element_type=F32)
        app[i] = (x[:NV] + x[NV:]).astype(BF)
    app_copy = pltpu.make_async_copy(app, app_ref, asem)
    app_copy.start()

    for copy in early:
        copy.wait()

    @pl.loop(count, KD - EARLY, step=2)
    def _(slot):
        late_copy(slot).wait()

    app_copy.wait()


def per_device(kernel_blocks, row_intersection, col_intersection, trial, coarse_of_row):
    hbm_spec = pl.BlockSpec(memory_space=pltpu.HBM)
    vmem_spec = pl.BlockSpec(memory_space=pltpu.VMEM)
    arrays = (coarse_of_row, kernel_blocks, col_intersection, trial, row_intersection)
    arrays = [pltpu.with_memory_space_constraint(x, pltpu.HBM) for x in arrays]
    begun, token = pl.pallas_call(
        begin,
        out_shape=(jax.ShapeDtypeStruct((KD, MD, S, S), BF), jax.ShapeDtypeStruct((8, 128), F32)),
        in_specs=[hbm_spec] * 4,
        out_specs=(hbm_spec, vmem_spec),
        scratch_shapes=[
            pltpu.SMEM((NCOL * KD,), jnp.int32),
            pltpu.VMEM((2, S, S), BF),
            pltpu.VMEM((MD, S, S), BF),
            pltpu.VMEM((BEGUN, S, S), BF),
            pltpu.VMEM((2, S, MD * S), BF),
            pltpu.VMEM((BEGUN, MD, S, S), BF),
            pltpu.SemaphoreType.DMA((4,)),
            pltpu.SemaphoreType.DMA((BEGUN // 2,)),
        ],
        compiler_params=pltpu.CompilerParams(vmem_limit_bytes=28 << 20),
        name="begin",
    )(arrays[0], arrays[1], arrays[2], arrays[4])
    early, right, rows, w = pl.pallas_call(
        exchange,
        out_shape=(
            jax.ShapeDtypeStruct((EARLY, MD, S, S), BF),
            jax.ShapeDtypeStruct((NB, S, MD * S), BF),
            jax.ShapeDtypeStruct((KD, S, S), BF),
            jax.ShapeDtypeStruct((2, 8, 8, S), F32),
        ),
        in_specs=[pl.BlockSpec(memory_space=pl.ANY)] + [hbm_spec] * 5,
        out_specs=(vmem_spec,) * 4,
        scratch_shapes=[
            pltpu.SMEM((NCOL * KD,), jnp.int32),
            pltpu.VMEM((NB, S, S), BF),
            pltpu.VMEM((NB, S, S), BF),
            pltpu.VMEM((MD, S, S), BF),
            pltpu.VMEM((MD, 4, S), BF),
            pltpu.VMEM((8, S), BF),
            pltpu.VMEM((8, 2, 8, S), BF),
            pltpu.VMEM((NB, NV, S), F32),
            pltpu.VMEM((NB, NV, S), BF),
            pltpu.VMEM((3, NEAR, S), BF),
            pltpu.VMEM((3, NEAR, S), BF),
            pltpu.VMEM((4, 2, NEAR, S), BF),
            pltpu.VMEM((NROW, 2, NV - NEAR, S), BF),
            pltpu.SemaphoreType.DMA((5,)),
            pltpu.SemaphoreType.DMA,
            pltpu.SemaphoreType.DMA,
            pltpu.SemaphoreType.DMA((NCOL,)),
            pltpu.SemaphoreType.DMA((8, 2)),
            pltpu.SemaphoreType.DMA((len(PARTS) + 1,)),
            pltpu.SemaphoreType.DMA((len(PARTS) + 1,)),
            pltpu.SemaphoreType.DMA((3,)),
            pltpu.SemaphoreType.DMA((4,)),
            pltpu.SemaphoreType.DMA((NROW,)),
            pltpu.SemaphoreType.DMA((NROW,)),
        ],
        compiler_params=pltpu.CompilerParams(
            collective_id=0, has_side_effects=True, vmem_limit_bytes=28 << 20
        ),
        name="exchange",
    )(token, *arrays)

    return pl.pallas_call(
        finish,
        out_shape=(jax.ShapeDtypeStruct((KD, MD, S, S), BF), jax.ShapeDtypeStruct((4, NV, S), BF)),
        in_specs=[hbm_spec] + [vmem_spec] * 4 + [hbm_spec],
        out_specs=(hbm_spec, hbm_spec),
        scratch_shapes=[
            pltpu.SMEM((NCOL * KD,), jnp.int32),
            pltpu.VMEM((KD - EARLY, MD, S, S), BF),
            pltpu.VMEM((4, NV, S), BF),
            pltpu.VMEM((2, 2 * NV, S), BF),
            pltpu.SemaphoreType.DMA,
            pltpu.SemaphoreType.DMA((EARLY // 2,)),
            pltpu.SemaphoreType.DMA(((KD - EARLY) // 2,)),
            pltpu.SemaphoreType.DMA,
        ],
        compiler_params=pltpu.CompilerParams(vmem_limit_bytes=28 << 20),
        input_output_aliases={5: 0},
        name="finish",
    )(arrays[0], early, right, rows, w, begun)


def solution(mesh):
    in_specs = (
        P("col", "row", None, None),
        P("col", None, None),
        P("row", None, None),
        P("row", "col", None),
        P(),
    )
    out_specs = (P("col", "row", None, None), P(("col", "row"), None, None))
    return jax.shard_map(
        per_device, mesh=mesh, in_specs=in_specs, out_specs=out_specs, check_vma=False
    )
```
